512 devices in a mesh: scen: 8 (over y), blk: 64 (over z, x, core).
Axes of the slice: x: 4, y: 8, z: 8, core: 2. Of those that a mesh axis runs over, the one named last changes fastest.
Arguments:
- returns: bfloat16 [512, 32768], P(('scen', 'blk')), may hold values from -6 to 6
- vol_hist: float32 [512, 32768], P(('scen', 'blk')), may hold values from 0.5 to 5.5, as said below
- vol_now: float32 [32768], replicated, may hold values from 0.5 to 2
- sensitivity: bfloat16 [16384, 128, 128], P('blk'), may hold values from -0.109375 to 0.109375
- block_pairs: int32 [16384, 3], P('blk'), may hold values from 0 to 255, as said below
- book_order: int32 [128], replicated, may hold values from 0 to 127, each once
Outputs:
- profit_loss: float32 [512, 16384], P('scen', 'blk')
- book_rms: float32 [16384], P('blk')
The draws below stay inside these ranges and needn't reach their ends.
Inputs may be any that keep to these rules, and one draw needn't show every extreme that they name: `block_pairs`: each index k of blk holds 256 slots; their factor blocks lie in k * 4 to k * 4 + 3; on each index the live slots come first; some index has all 256 slots live. `vol_hist`: positive volatilities.
All inputs are finite; a program needn't handle non-finite values.
Results may differ from the reference program's by a relative error of at most 0.0029.
Values may be sent and summed in bfloat16 or wider, within the bound.
A program may use at most 64 MiB of HBM per device.

```python
import math
import jax
import jax.numpy as jnp
from jax import lax

BS = 128
FB_DEV = 4
BLK_DEV = 256
NFB = 256
NBB = 128
F = 32768
SLOTS = 16384
S = 512
N_BLK = 64


def draw_vol_hist(key, part):
    rows = jnp.arange(S, dtype=jnp.float32) / S
    base = jnp.exp(jax.random.uniform(key, (S, F), jnp.float32, jnp.log(0.5), jnp.log(2.0)))
    ramp = 0.7
    return base * jnp.exp(ramp * rows)[:, None]


def draw_block_pairs(key, part):
    devices = NFB // FB_DEV
    key_count = jax.random.fold_in(key, 11)
    key_full = jax.random.fold_in(key, 12)
    key_factor = jax.random.fold_in(key, 13)
    key_book = jax.random.fold_in(key, 14)
    counts = jax.random.randint(key_count, (devices,), BLK_DEV // 4, BLK_DEV // 2 + 1)
    full_device = jax.random.randint(key_full, (), 0, devices)
    counts = jnp.where(jnp.arange(devices) == full_device, BLK_DEV, counts)
    slot_index = jnp.arange(BLK_DEV, dtype=jnp.int32)
    live = (slot_index[None, :] < counts[:, None]).astype(jnp.int32)
    factor = jnp.arange(devices, dtype=jnp.int32)[:, None] * FB_DEV + jax.random.randint(key_factor, (devices, BLK_DEV), 0, FB_DEV)
    book = jax.random.randint(key_book, (devices, BLK_DEV), 0, NBB)
    stacked = jnp.stack([factor.astype(jnp.int32), book.astype(jnp.int32), live], axis=-1)
    return stacked.reshape(devices * BLK_DEV, 3)


def levels(own_key, dims, pieces, low, high):
    def one(axis_at, parts):
        steps = jax.random.uniform(jax.random.fold_in(jax.random.fold_in(own_key, 6), axis_at), (parts,), jnp.float32, low / len(pieces), high / len(pieces))
        return jnp.repeat(jnp.exp(steps), dims[axis_at] // parts).reshape((-1,) + (1,) * (len(dims) - axis_at - 1))

    loudness = one(*pieces[0])
    for cut in pieces[1:]:
        loudness = loudness * one(*cut)
    return loudness


def scatter_about(own_key, extent, deviation, reach, pieces=(), held_as=jnp.bfloat16):
    entries = jax.random.normal(own_key, extent, jnp.float32) * deviation
    if len(pieces) > 0:
        entries = levels(own_key, extent, pieces, -0.22, 0.18) * entries
    return jnp.clip(entries, min=-reach, max=reach).astype(held_as)


def setup_inputs(seed: int = 0) -> dict:
    arg_keys = jax.random.split(jax.random.key(seed), 7)
    returns = scatter_about(arg_keys[0], (S, F), 1.0, 6.0, ((0, 512),))
    vol_hist = draw_vol_hist(jax.random.fold_in(arg_keys[6], 71), 0)
    vol_now = jnp.clip(jnp.exp(jax.random.uniform(arg_keys[2], (F,), jnp.float32, math.log(0.5), math.log(2.0))), 0.5, 2.0)
    sensitivity = scatter_about(arg_keys[3], (SLOTS, BS, BS), (BS * 24) ** -0.5, 0.109375, ((0, 64),))
    block_pairs = draw_block_pairs(jax.random.fold_in(arg_keys[6], 71), 0)
    book_order = jax.random.permutation(arg_keys[5], NBB).astype(jnp.int32)
    return {"returns": returns, "vol_hist": vol_hist, "vol_now": vol_now, "sensitivity": sensitivity, "block_pairs": block_pairs, "book_order": book_order}


def reference(returns, vol_hist, vol_now, sensitivity, block_pairs, book_order):
    rescaled = (returns.astype(jnp.float32) * vol_now[None, :] / vol_hist).astype(jnp.bfloat16)
    shock_blocks = rescaled.reshape(S, NFB, BS)
    order_index = jnp.arange(NBB, dtype=jnp.int32)
    position_of = jnp.zeros((NBB,), jnp.int32).at[book_order].set(order_index)
    sens_groups = sensitivity.reshape(N_BLK, BLK_DEV, BS, BS)
    pair_groups = block_pairs.reshape(N_BLK, BLK_DEV, 3)

    def add_group(total, group):
        sens_group, pair_group = group
        picked = jnp.take(shock_blocks, pair_group[:, 0], axis=1)
        products = jnp.einsum('skc,kcd->ksd', picked.astype(jnp.float32), sens_group.astype(jnp.float32))
        products = products * pair_group[:, 2].astype(jnp.float32)[:, None, None]
        target = position_of[pair_group[:, 1]]
        return (total + jax.ops.segment_sum(products, target, num_segments=NBB), None)
    start_total = jnp.zeros((NBB, S, BS), jnp.float32)
    total, _ = lax.scan(add_group, start_total, (sens_groups, pair_groups))
    profit_loss = total.transpose(1, 0, 2).reshape(S, NBB * BS)
    book_rms = jnp.sqrt(lax.optimization_barrier(jnp.sum(profit_loss * profit_loss, axis=0)) / S + 1e-06)
    return (profit_loss, book_rms)
```

```python
import functools

import jax
import jax.numpy as jnp
from jax import lax
from jax.experimental import pallas as pl
from jax.experimental.pallas import tpu as pltpu
from jax.sharding import PartitionSpec as P

MESH = pl.DeviceIdType.MESH
F32 = jnp.float32
BF16 = jnp.bfloat16
NX = 4
NC = 2
LANES = 128


def remote(src, dst, send, recv, **where):
    return pltpu.make_async_remote_copy(
        src_ref=src, dst_ref=dst, send_sem=send, recv_sem=recv, device_id=where, device_id_type=MESH
    )


def iota(shape, axis):
    return lax.broadcasted_iota(jnp.int32, shape, axis).astype(F32)


def to_column(row):
    n = row.shape[1]
    eye = lax.broadcasted_iota(jnp.int32, (n, n), 0) == lax.broadcasted_iota(jnp.int32, (n, n), 1)
    return jnp.sum(jnp.where(eye, jnp.broadcast_to(row, (n, n)), 0.0), axis=1, keepdims=True)


def sort_slots(pairs, order, first_factor):
    slots, blocks = pairs.shape[1], order.shape[1]
    pairs = pairs.astype(F32)
    factor = pairs[0:1] - first_factor.astype(F32)
    matches = to_column(order.astype(F32)) == pairs[1:2]
    position = jnp.sum(jnp.where(matches, iota((blocks, slots), 0), 0.0), axis=0, keepdims=True)
    position = jnp.where(pairs[2:3] > 0.5, position, float(blocks))
    value = (position * slots + iota((1, slots), 1)) * 4.0 + factor
    value_col = to_column(value)
    position_col = to_column(position)
    rank_col = jnp.sum(jnp.where(value < value_col, 1.0, 0.0), axis=1, keepdims=True)
    ordered = jnp.sum(jnp.where(rank_col == iota((slots, slots), 1), value_col, 0.0), axis=0, keepdims=True)
    columns = iota((slots, blocks), 1)
    upto = jnp.sum(jnp.where(position_col <= columns, 1.0, 0.0), axis=0, keepdims=True)
    here = jnp.sum(jnp.where(position_col == columns, 1.0, 0.0), axis=0, keepdims=True)
    last = jnp.maximum(upto - 1.0, 0.0) * 2.0 + jnp.minimum(here, 1.0)
    return ordered.astype(jnp.int32), last.astype(jnp.int32)


def kernel(
    ny, nz, dz_order,
    row_ref, pairs_ref, order_ref, sens_ref,
    out_ref, rms_ref,
    sens_v, land1, turned, shocks_f, shocks_b, running, give, got0, part_x, got1, part_z, got2, mine,
    squares, got3, ordered_v, last_v, ordered_s, last_s,
    sens_sem, meta_sem, send1, recv1, send2, recv2, send_c, recv_c, send_x, recv_x, send_z, recv_z, send_y, recv_y,
):
    nq = NX * NC
    slots = sens_v.shape[0]
    rows = nz * nq
    me_y = lax.axis_index("scen")
    me = lax.axis_index("blk")
    z, q = me // nq, me % nq
    x, c = q // NC, q % NC
    fb = shocks_f.shape[1]

    pieces = sens_sem.shape[0]
    each = slots // pieces
    loads = [
        pltpu.make_async_copy(sens_ref.at[pl.ds(i * each, each)], sens_v.at[pl.ds(i * each, each)], sens_sem.at[i])
        for i in range(pieces)
    ]
    for load in loads:
        load.start()

    barrier = pltpu.get_barrier_semaphore()
    for d in range(1, nz):
        pl.semaphore_signal(barrier, 1, device_id={"blk": lax.rem(z + d, nz) * nq + q}, device_id_type=MESH)
    for d in range(1, nq):
        pl.semaphore_signal(barrier, 1, device_id={"blk": z * nq + lax.rem(q + d, nq)}, device_id_type=MESH)
    for d in range(1, ny):
        pl.semaphore_signal(barrier, 1, device_id={"scen": lax.rem(me_y + d, ny)}, device_id_type=MESH)
    pl.semaphore_wait(barrier, nz - 1 + nq - 1 + ny - 1)

    slab = nq * fb
    stage1 = []
    for d in range(1, nz):
        to = lax.rem(z + d, nz)
        stage1.append(
            remote(row_ref.at[to], land1.at[z], send1.at[d - 1], recv1.at[d - 1], blk=to * nq + q)
        )
    for copy in stage1:
        copy.start()
    land1[pl.ds(z, 1)] = row_ref[pl.ds(z, 1)]

    ordered, last = sort_slots(pairs_ref[...], order_ref[...], me * fb)
    ordered_v[...] = ordered
    last_v[...] = last
    metas = [
        pltpu.make_async_copy(ordered_v, ordered_s, meta_sem.at[0]),
        pltpu.make_async_copy(last_v, last_s, meta_sem.at[1]),
    ]
    for copy in metas:
        copy.start()

    for copy in stage1:
        copy.wait_recv()
    turned[...] = jnp.swapaxes(land1[...].astype(F32), 0, 1).reshape(nq, fb, nz, LANES)
    stage2 = []
    for d in range(1, nq):
        to = lax.rem(q + d, nq)
        stage2.append(
            remote(turned.at[to], shocks_f.at[q], send2.at[d - 1], recv2.at[d - 1], blk=z * nq + to)
        )
    for copy in stage2:
        copy.start()
    shocks_f[pl.ds(q, 1)] = turned[pl.ds(q, 1)]
    for copy in metas:
        copy.wait()
    for load in loads:
        load.wait()
    for copy in stage2:
        copy.wait_recv()
    for f in range(fb):
        shocks_b[f] = shocks_f[:, f].reshape(rows, LANES).astype(BF16)

    unroll = 8
    slot_bits = slots.bit_length() - 1

    def slot_group(g, carry):
        total, before = carry
        for u in range(unroll):
            j = g * unroll + u
            value = ordered_s[0, j]
            factor = value & 3
            k = (value >> 2) & (slots - 1)
            position = value >> (2 + slot_bits)
            product = jnp.dot(shocks_b[factor], sens_v[k], preferred_element_type=F32)
            same = (position == before).astype(F32)
            total = total * same + product
            running[j] = total
            before = position
        return total, before

    lax.fori_loop(0, slots // unroll, slot_group, (jnp.zeros((rows, LANES), F32), jnp.int32(-1)))

    def partial_of(p):
        value = last_s[0, p]
        return running[(value >> 1) & (slots - 1)] * (value & 1).astype(F32)

    chunks = len(dz_order)
    core_copies, x_copies, z_copies = [], [], []
    for i, dz in enumerate(dz_order):
        to_z = lax.rem(z + dz, nz)
        for to_x in range(NX):
            for h in range(2):
                give[i, to_x, h] = partial_of(((to_z * NX + to_x) * NC + (1 - c)) * 2 + h)
        copy = remote(give.at[i], got0.at[i], send_c.at[i], recv_c.at[i], blk=z * nq + x * NC + (1 - c))
        copy.start()
        core_copies.append(copy)

    for i in range(chunks + 1):
        if i < chunks:
            dz = dz_order[i]
            to_z = lax.rem(z + dz, nz)
            core_copies[i].wait_recv()
            group = []
            for d in range(NX):
                to_x = lax.rem(x + d, NX)
                for h in range(2):
                    total = got0[i, to_x, h] + partial_of(((to_z * NX + to_x) * NC + c) * 2 + h)
                    if d == 0:
                        mine[i % 2, h] = total
                    else:
                        part_x[i, d - 1, h] = total.astype(BF16)
                if d > 0:
                    copy = remote(
                        part_x.at[i, d - 1], got1.at[i, d - 1], send_x.at[i, d - 1], recv_x.at[i, d - 1],
                        blk=(z * NX + to_x) * NC + c,
                    )
                    copy.start()
                    group.append(copy)
            x_copies.append(group)
        if i > 0:
            e = i - 1
            dz = dz_order[e]
            for copy in x_copies[e]:
                copy.wait_recv()
            for h in range(2):
                total = mine[e % 2, h]
                for d in range(NX - 1):
                    total = total + got1[e, d, h].astype(F32)
                if dz == 0:
                    mine[e % 2, h] = total
                else:
                    part_z[e, h] = total.astype(BF16)
            if dz != 0:
                copy = remote(
                    part_z.at[e], got2.at[e], send_z.at[e], recv_z.at[e],
                    blk=lax.rem(z + dz, nz) * nq + q,
                )
                copy.start()
                z_copies.append(copy)
    for copy in z_copies:
        copy.wait_recv()
    for h in range(2):
        total = mine[(chunks - 1) % 2, h]
        for e in range(chunks - 1):
            total = total + got2[e, h].astype(F32)
        squares[0, h:h + 1] = jnp.sum(total * total, axis=0, keepdims=True)
        total = jnp.swapaxes(total.reshape(nq, nz, LANES), 0, 1)
        out_ref[:, h * LANES:(h + 1) * LANES] = total.reshape(rows, LANES)
    y_copies = []
    for d in range(1, ny):
        copy = remote(
            squares.at[0], got3.at[d - 1], send_y.at[d - 1], recv_y.at[d - 1], scen=lax.rem(me_y + d, ny)
        )
        copy.start()
        y_copies.append(copy)
    for copy in y_copies:
        copy.wait_recv()
    total = squares[0]
    for d in range(ny - 1):
        total = total + got3[d]
    rms_ref[...] = jnp.sqrt(total / (rows * ny) + 1e-06)
    for copy in stage1 + stage2 + core_copies + z_copies + y_copies:
        copy.wait_send()
    for group in x_copies:
        for copy in group:
            copy.wait_send()


def shards(ny, nz, returns, vol_hist, vol_now, sensitivity, block_pairs, book_order):
    rescaled = (returns.astype(F32) * vol_now[None, :] / vol_hist).astype(BF16)
    nq = NX * NC
    slots = sensitivity.shape[0]
    blocks = book_order.shape[0]
    fb = rescaled.shape[1] // (nz * nq * LANES)
    rows = nz * nq
    row = rescaled.reshape(nz, nq * fb, LANES)
    near = sorted(range(nz), key=lambda d: (-min(d, nz - d), d))
    dma = pltpu.SemaphoreType.DMA
    vm = pltpu.VMEM
    block = (rows, LANES)
    out, rms = pl.pallas_call(
        functools.partial(kernel, ny, nz, near),
        out_shape=(
            jax.ShapeDtypeStruct((rows, 2 * LANES), F32),
            jax.ShapeDtypeStruct((2, LANES), F32),
        ),
        in_specs=[
            pl.BlockSpec(memory_space=pltpu.VMEM),
            pl.BlockSpec(memory_space=pltpu.VMEM),
            pl.BlockSpec(memory_space=pltpu.VMEM),
            pl.BlockSpec(memory_space=pl.ANY),
        ],
        out_specs=(pl.BlockSpec(memory_space=pltpu.VMEM), pl.BlockSpec(memory_space=pltpu.VMEM)),
        scratch_shapes=[
            vm((slots, LANES, LANES), BF16),
            vm((nz, nq * fb, LANES), BF16),
            vm((nq, fb, nz, LANES), F32),
            vm((nq, fb, nz, LANES), F32),
            vm((fb,) + block, BF16),
            vm((slots,) + block, F32),
            vm((nz, NX, 2) + block, F32),
            vm((nz, NX, 2) + block, F32),
            vm((nz, NX - 1, 2) + block, BF16),
            vm((nz, NX - 1, 2) + block, BF16),
            vm((nz - 1, 2) + block, BF16),
            vm((nz - 1, 2) + block, BF16),
            vm((2, 2) + block, F32),
            vm((1, 2, LANES), F32),
            vm((ny - 1, 2, LANES), F32),
            vm((1, slots), jnp.int32),
            vm((1, blocks), jnp.int32),
            pltpu.SMEM((1, slots), jnp.int32),
            pltpu.SMEM((1, blocks), jnp.int32),
            dma((8,)),
            dma((2,)),
            dma((nz - 1,)),
            dma((nz - 1,)),
            dma((nq - 1,)),
            dma((nq - 1,)),
            dma((nz,)),
            dma((nz,)),
            dma((nz, NX - 1)),
            dma((nz, NX - 1)),
            dma((nz - 1,)),
            dma((nz - 1,)),
            dma((ny - 1,)),
            dma((ny - 1,)),
        ],
        compiler_params=pltpu.CompilerParams(
            collective_id=0, has_side_effects=True, vmem_limit_bytes=48 << 20
        ),
        name="profit_loss",
    )(row, block_pairs.T, book_order.reshape(1, blocks), sensitivity)
    return out, rms.reshape(2 * LANES)


def solution(mesh):
    ny, nb = mesh.shape["scen"], mesh.shape["blk"]
    return jax.shard_map(
        functools.partial(shards, ny, nb // (NX * NC)),
        mesh=mesh,
        in_specs=(
            P(("scen", "blk"), None),
            P(("scen", "blk"), None),
            P(),
            P("blk", None, None),
            P("blk", None),
            P(),
        ),
        out_specs=(P("scen", "blk"), P("blk")),
        check_vma=False,
    )
```

```python
import functools

import jax
import jax.numpy as jnp
from jax import lax
from jax.experimental import pallas as pl
from jax.experimental.pallas import tpu as pltpu
from jax.sharding import PartitionSpec as P

MESH = pl.DeviceIdType.MESH
F32 = jnp.float32
BF16 = jnp.bfloat16
NX = 4
NC = 2
LANES = 128


def remote(src, dst, send, recv, **where):
    return pltpu.make_async_remote_copy(
        src_ref=src, dst_ref=dst, send_sem=send, recv_sem=recv, device_id=where, device_id_type=MESH
    )


def far_first(n):
    return sorted(range(1, n), key=lambda d: (-min(d, n - d), d))


def iota(shape, axis):
    return lax.broadcasted_iota(jnp.int32, shape, axis).astype(F32)


def to_column(row):
    n = row.shape[1]
    eye = lax.broadcasted_iota(jnp.int32, (n, n), 0) == lax.broadcasted_iota(jnp.int32, (n, n), 1)
    return jnp.sum(jnp.where(eye, jnp.broadcast_to(row, (n, n)), 0.0), axis=1, keepdims=True)


def sort_slots(pairs, order, first_factor):
    slots, blocks = pairs.shape[1], order.shape[1]
    pairs = pairs.astype(F32)
    factor = pairs[0:1] - first_factor.astype(F32)
    matches = to_column(order.astype(F32)) == pairs[1:2]
    position = jnp.sum(jnp.where(matches, iota((blocks, slots), 0), 0.0), axis=0, keepdims=True)
    position = jnp.where(pairs[2:3] > 0.5, position, float(blocks))
    value = (position * slots + iota((1, slots), 1)) * 4.0 + factor
    value_col = to_column(value)
    position_col = to_column(position)
    rank_col = jnp.sum(jnp.where(value < value_col, 1.0, 0.0), axis=1, keepdims=True)
    ordered = jnp.sum(jnp.where(rank_col == iota((slots, slots), 1), value_col, 0.0), axis=0, keepdims=True)
    columns = iota((slots, blocks), 1)
    upto = jnp.sum(jnp.where(position_col <= columns, 1.0, 0.0), axis=0, keepdims=True)
    here = jnp.sum(jnp.where(position_col == columns, 1.0, 0.0), axis=0, keepdims=True)
    last = jnp.maximum(upto - 1.0, 0.0) * 2.0 + jnp.minimum(here, 1.0)
    return ordered.astype(jnp.int32), last.astype(jnp.int32)


def kernel(
    ny, nz, dz_order,
    returns_ref, hist_ref, now_ref, pairs_ref, order_ref, sens_ref,
    out_ref, rms_ref,
    returns_v, hist_v, now_v, pairs_v, order_v, wide, row_ref,
    sens_v, land1, gathered, shocks_b, running, give, got0, part_r, got_r, held, part_x, got1, part_z, got2, mine,
    squares, got3, ordered_v, last_v, ordered_s, last_s,
    in_sem, sens_sem, meta_sem, send1, recv1, send2, recv2, send_c, recv_c, send_r, recv_r, send_x, recv_x, send_z, recv_z, send_y, recv_y,
):
    nq = NX * NC
    slots = sens_v.shape[0]
    rows = nz * nq
    me_y = lax.axis_index("scen")
    me = lax.axis_index("blk")
    z, q = me // nq, me % nq
    x, c = q // NC, q % NC
    fb = shocks_b.shape[0]

    barrier = pltpu.get_barrier_semaphore()
    for d in far_first(nz):
        pl.semaphore_signal(barrier, 1, device_id={"blk": lax.rem(z + d, nz) * nq + q}, device_id_type=MESH)
    for d in far_first(ny):
        pl.semaphore_signal(barrier, 1, device_id={"scen": lax.rem(me_y + d, ny)}, device_id_type=MESH)
    for d in range(1, nq):
        pl.semaphore_signal(barrier, 1, device_id={"blk": z * nq + lax.rem(q + d, nq)}, device_id_type=MESH)

    inputs = [
        pltpu.make_async_copy(src, dst, in_sem.at[i])
        for i, (src, dst) in enumerate((
            (returns_ref, returns_v), (hist_ref, hist_v), (now_ref, now_v), (pairs_ref, pairs_v), (order_ref, order_v)
        ))
    ]
    for copy in inputs:
        copy.start()
    pieces = sens_sem.shape[0]
    each = slots // pieces
    loads = [
        pltpu.make_async_copy(sens_ref.at[pl.ds(i * each, each)], sens_v.at[pl.ds(i * each, each)], sens_sem.at[i])
        for i in range(pieces)
    ]
    for copy in inputs:
        copy.wait()
    for load in loads:
        load.start()

    for i in range(rows * fb):
        wide[i // fb, i % fb:i % fb + 1] = returns_v[:, i * LANES:(i + 1) * LANES].astype(F32)
    row_ref[...] = (wide[...] * now_v[...] / hist_v[...]).astype(BF16).reshape(nz, nq, fb, LANES)

    pl.semaphore_wait(barrier, nz - 1 + nq - 1 + ny - 1)

    stage1 = []
    for d in far_first(nz):
        to = lax.rem(z + d, nz)
        copy = remote(row_ref.at[to], land1.at[z], send1.at[d - 1], recv1.at[d - 1], blk=to * nq + q)
        copy.start()
        stage1.append(copy)
    land1[pl.ds(z, 1)] = row_ref[pl.ds(z, 1)]

    ordered, last = sort_slots(pairs_v[...], order_v[...], me * fb)
    ordered_v[...] = ordered
    last_v[...] = last
    metas = [
        pltpu.make_async_copy(ordered_v, ordered_s, meta_sem.at[0]),
        pltpu.make_async_copy(last_v, last_s, meta_sem.at[1]),
    ]
    for copy in metas:
        copy.start()

    for copy in stage1:
        copy.wait_recv()
    stage2 = []
    for d in (4, 3, 5, 2, 6, 1, 7)[:] if nq == 8 else range(1, nq):
        to = lax.rem(q + d, nq)
        copy = remote(land1.at[:, to], gathered.at[q], send2.at[d - 1], recv2.at[d - 1], blk=z * nq + to)
        copy.start()
        stage2.append(copy)
    gathered[pl.ds(q, 1)] = land1[:, pl.ds(q, 1)].reshape(1, nz, fb, LANES)
    for copy in metas:
        copy.wait()
    for load in loads:
        load.wait()
    for copy in stage2:
        copy.wait_recv()
    by_factor = jnp.swapaxes(gathered[...].reshape(rows, fb, LANES).astype(F32), 0, 1)
    shocks_b[...] = by_factor.astype(BF16)

    unroll = min(32, slots)
    slot_bits = slots.bit_length() - 1

    def slot_group(g, carry):
        total, before = carry
        for u in range(unroll):
            j = g * unroll + u
            value = ordered_s[0, j]
            factor = value & 3
            k = (value >> 2) & (slots - 1)
            position = value >> (2 + slot_bits)
            product = jnp.dot(shocks_b[factor], sens_v[k], preferred_element_type=F32)
            same = (position == before).astype(F32)
            total = total * same + product
            running[j] = total
            before = position
        return total, before

    lax.fori_loop(0, slots // unroll, slot_group, (jnp.zeros((rows, LANES), F32), jnp.int32(-1)))

    def partial_of(p):
        value = last_s[0, p]
        return running[(value >> 1) & (slots - 1)] * (value & 1).astype(F32)

    chunks = len(dz_order)
    core_copies, x_copies, z_copies = [], [], []
    for i, dz in enumerate(dz_order):
        to_z = lax.rem(z + dz, nz)
        for to_x in range(NX):
            for h in range(2):
                give[i, to_x, h] = partial_of(((to_z * NX + to_x) * NC + (1 - c)) * 2 + h)
        copy = remote(give.at[i], got0.at[i], send_c.at[i], recv_c.at[i], blk=z * nq + x * NC + (1 - c))
        copy.start()
        core_copies.append(copy)

    right = (z * NX + lax.rem(x + 1, NX)) * NC + c
    left = (z * NX + lax.rem(x + NX - 1, NX)) * NC + c
    relays = []
    for i, dz in enumerate(dz_order):
        to_z = lax.rem(z + dz, nz)
        core_copies[i].wait_recv()
        pair = []
        for d in (2, 1, 3, 0):
            to_x = lax.rem(x + d, NX)
            for h in range(2):
                total = got0[i, to_x, h] + partial_of(((to_z * NX + to_x) * NC + c) * 2 + h)
                if d == 0:
                    mine[i, h] = total
                elif d == 2:
                    part_r[i, h] = total.astype(BF16)
                    copy = remote(
                        part_r.at[i, h], got_r.at[i, h], send_r.at[i, h], recv_r.at[i, h], blk=left if h else right
                    )
                    copy.start()
                    pair.append(copy)
                else:
                    held[i, d // 2, h] = total
        relays.append(pair)

    for i in range(chunks):
        for copy in relays[i]:
            copy.wait_recv()
        group = []
        for way in range(2):
            for h in range(2):
                total = held[i, way, h]
                if h == way:
                    total = total + got_r[i, h].astype(F32)
                part_x[i, way, h] = total.astype(BF16)
            copy = remote(
                part_x.at[i, way], got1.at[i, way], send_x.at[i, way], recv_x.at[i, way], blk=left if way else right
            )
            copy.start()
            group.append(copy)
        x_copies.append(group)

    for i, dz in enumerate(dz_order):
        for copy in x_copies[i]:
            copy.wait_recv()
        for h in range(2):
            total = mine[i, h]
            for way in range(2):
                total = total + got1[i, way, h].astype(F32)
            if dz == 0:
                mine[i, h] = total
            else:
                part_z[i, h] = total.astype(BF16)
        if dz != 0:
            copy = remote(
                part_z.at[i], got2.at[i], send_z.at[i], recv_z.at[i], blk=lax.rem(z + dz, nz) * nq + q
            )
            copy.start()
            z_copies.append(copy)
    for copy in z_copies:
        copy.wait_recv()
    for h in range(2):
        total = mine[chunks - 1, h]
        for e in range(chunks - 1):
            total = total + got2[e, h].astype(F32)
        squares[0, h:h + 1] = jnp.sum(total * total, axis=0, keepdims=True)
        total = jnp.swapaxes(total.reshape(nq, nz, LANES), 0, 1)
        out_ref[:, h * LANES:(h + 1) * LANES] = total.reshape(rows, LANES)
    y_copies = []
    for d in far_first(ny):
        copy = remote(
            squares.at[0], got3.at[d - 1], send_y.at[d - 1], recv_y.at[d - 1], scen=lax.rem(me_y + d, ny)
        )
        copy.start()
        y_copies.append(copy)
    for copy in y_copies:
        copy.wait_recv()
    total = squares[0]
    for d in range(ny - 1):
        total = total + got3[d]
    rms_ref[...] = jnp.sqrt(total / (rows * ny) + 1e-06)
    for copy in stage1 + stage2 + core_copies + z_copies + y_copies:
        copy.wait_send()
    for group in relays + x_copies:
        for copy in group:
            copy.wait_send()


def shards(ny, nz, returns, vol_hist, vol_now, sensitivity, block_pairs, book_order):
    nq = NX * NC
    slots = sensitivity.shape[0]
    blocks = book_order.shape[0]
    factors = returns.shape[1]
    rows = nz * nq
    fb = factors // (rows * LANES)
    wide = (rows, fb, LANES)
    dma = pltpu.SemaphoreType.DMA
    vm = pltpu.VMEM
    block = (rows, LANES)
    out, rms = pl.pallas_call(
        functools.partial(kernel, ny, nz, far_first(nz) + [0]),
        out_shape=(
            jax.ShapeDtypeStruct((rows, 2 * LANES), F32),
            jax.ShapeDtypeStruct((2, LANES), F32),
        ),
        in_specs=[pl.BlockSpec(memory_space=pltpu.HBM)] * 6,
        out_specs=(pl.BlockSpec(memory_space=pltpu.VMEM), pl.BlockSpec(memory_space=pltpu.VMEM)),
        scratch_shapes=[
            vm((1, factors), BF16),
            vm(wide, F32),
            vm(wide, F32),
            vm((3, slots), jnp.int32),
            vm((1, blocks), jnp.int32),
            vm(wide, F32),
            vm((nz, nq, fb, LANES), BF16),
            vm((slots, LANES, LANES), BF16),
            vm((nz, nq, fb, LANES), BF16),
            vm((nq, nz, fb, LANES), BF16),
            vm((fb,) + block, BF16),
            vm((slots,) + block, F32),
            vm((nz, NX, 2) + block, F32),
            vm((nz, NX, 2) + block, F32),
            vm((nz, 2) + block, BF16),
            vm((nz, 2) + block, BF16),
            vm((nz, 2, 2) + block, F32),
            vm((nz, 2, 2) + block, BF16),
            vm((nz, 2, 2) + block, BF16),
            vm((nz - 1, 2) + block, BF16),
            vm((nz - 1, 2) + block, BF16),
            vm((nz, 2) + block, F32),
            vm((1, 2, LANES), F32),
            vm((ny - 1, 2, LANES), F32),
            vm((1, slots), jnp.int32),
            vm((1, blocks), jnp.int32),
            pltpu.SMEM((1, slots), jnp.int32),
            pltpu.SMEM((1, blocks), jnp.int32),
            dma((5,)),
            dma((8,)),
            dma((2,)),
            dma((nz - 1,)),
            dma((nz - 1,)),
            dma((nq - 1,)),
            dma((nq - 1,)),
            dma((nz,)),
            dma((nz,)),
            dma((nz, 2)),
            dma((nz, 2)),
            dma((nz, 2)),
            dma((nz, 2)),
            dma((nz - 1,)),
            dma((nz - 1,)),
            dma((ny - 1,)),
            dma((ny - 1,)),
        ],
        compiler_params=pltpu.CompilerParams(
            collective_id=0, has_side_effects=True, vmem_limit_bytes=60 << 20
        ),
        name="profit_loss",
    )(
        returns, vol_hist.reshape(wide), vol_now.reshape(wide), block_pairs.T, book_order.reshape(1, blocks), sensitivity
    )
    return out, rms.reshape(2 * LANES)


def solution(mesh):
    ny, nb = mesh.shape["scen"], mesh.shape["blk"]
    return jax.shard_map(
        functools.partial(shards, ny, nb // (NX * NC)),
        mesh=mesh,
        in_specs=(
            P(("scen", "blk"), None),
            P(("scen", "blk"), None),
            P(),
            P("blk", None, None),
            P("blk", None),
            P(),
        ),
        out_specs=(P("scen", "blk"), P("blk")),
        check_vma=False,
    )
```

```python
import functools

import jax
import jax.numpy as jnp
from jax import lax
from jax.experimental import pallas as pl
from jax.experimental.pallas import tpu as pltpu
from jax.sharding import PartitionSpec as P

MESH = pl.DeviceIdType.MESH
F32 = jnp.float32
BF16 = jnp.bfloat16
NX = 4
NC = 2
LANES = 128


def remote(src, dst, send, recv, **where):
    return pltpu.make_async_remote_copy(
        src_ref=src, dst_ref=dst, send_sem=send, recv_sem=recv, device_id=where, device_id_type=MESH
    )


def far_first(n):
    return sorted(range(1, n), key=lambda d: (-min(d, n - d), d))


def iota(shape, axis):
    return lax.broadcasted_iota(jnp.int32, shape, axis).astype(F32)


def to_column(row):
    n = row.shape[1]
    eye = lax.broadcasted_iota(jnp.int32, (n, n), 0) == lax.broadcasted_iota(jnp.int32, (n, n), 1)
    return jnp.sum(jnp.where(eye, jnp.broadcast_to(row, (n, n)), 0.0), axis=1, keepdims=True)


def sort_slots(pairs, order, first_factor):
    slots, blocks = pairs.shape[1], order.shape[1]
    pairs = pairs.astype(F32)
    factor = pairs[0:1] - first_factor.astype(F32)
    matches = to_column(order.astype(F32)) == pairs[1:2]
    position = jnp.sum(jnp.where(matches, iota((blocks, slots), 0), 0.0), axis=0, keepdims=True)
    position = jnp.where(pairs[2:3] > 0.5, position, float(blocks))
    value = (position * slots + iota((1, slots), 1)) * 4.0 + factor
    value_col = to_column(value)
    position_col = to_column(position)
    rank_col = jnp.sum(jnp.where(value < value_col, 1.0, 0.0), axis=1, keepdims=True)
    ordered = jnp.sum(jnp.where(rank_col == iota((slots, slots), 1), value_col, 0.0), axis=0, keepdims=True)
    columns = iota((slots, blocks), 1)
    upto = jnp.sum(jnp.where(position_col <= columns, 1.0, 0.0), axis=0, keepdims=True)
    here = jnp.sum(jnp.where(position_col == columns, 1.0, 0.0), axis=0, keepdims=True)
    last = jnp.maximum(upto - 1.0, 0.0) * 2.0 + jnp.minimum(here, 1.0)
    return ordered.astype(jnp.int32), last.astype(jnp.int32)


def kernel(
    ny, nz, dz_order,
    returns_ref, hist_ref, now_ref, pairs_ref, order_ref, sens_ref,
    out_hbm, rms_hbm,
    out_ref, rms_ref, returns_v, hist_v, now_v, pairs_v, order_v, wide, row_ref,
    sens_v, land1, gathered, shocks_b, running, give, got0, part_r, got_r, held, part_x, got1, part_z, got2, mine, rest_z, got_v, rest_own, rest_mine, rest_x, got_w,
    squares, got3, ordered_v, last_v, ordered_s, last_s,
    in_sem, out_sem, sens_sem, meta_sem, send1, recv1, send2, recv2, send_c, recv_c, send_r, recv_r, send_x, recv_x, send_z, recv_z, send_v, recv_v, send_w, recv_w, send_y, recv_y,
):
    nq = NX * NC
    slots = sens_v.shape[0]
    rows = nz * nq
    me_y = lax.axis_index("scen")
    me = lax.axis_index("blk")
    z, q = me // nq, me % nq
    x, c = q // NC, q % NC
    fb = shocks_b.shape[0]

    inputs = [
        pltpu.make_async_copy(src, dst, in_sem.at[i])
        for i, (src, dst) in enumerate((
            (returns_ref, returns_v), (hist_ref, hist_v), (now_ref, now_v), (pairs_ref, pairs_v), (order_ref, order_v)
        ))
    ]
    for copy in inputs:
        copy.start()
    barrier = pltpu.get_barrier_semaphore()
    for d in far_first(nz):
        pl.semaphore_signal(barrier, 1, device_id={"blk": lax.rem(z + d, nz) * nq + q}, device_id_type=MESH)
    for d in far_first(ny):
        pl.semaphore_signal(barrier, 1, device_id={"scen": lax.rem(me_y + d, ny)}, device_id_type=MESH)
    for d in range(1, nq):
        pl.semaphore_signal(barrier, 1, device_id={"blk": z * nq + lax.rem(q + d, nq)}, device_id_type=MESH)

    pieces = sens_sem.shape[0]
    each = slots // pieces
    loads = [
        pltpu.make_async_copy(sens_ref.at[pl.ds(i * each, each)], sens_v.at[pl.ds(i * each, each)], sens_sem.at[i])
        for i in range(pieces)
    ]
    for copy in inputs:
        copy.wait()
    for load in loads:
        load.start()

    for i in range(rows * fb):
        wide[i // fb, i % fb:i % fb + 1] = returns_v[:, i * LANES:(i + 1) * LANES].astype(F32)
    row_ref[...] = (wide[...] * now_v[...] / hist_v[...]).astype(BF16).reshape(nz, nq, fb, LANES)

    pl.semaphore_wait(barrier, nz - 1 + nq - 1 + ny - 1)

    stage1 = []
    for d in far_first(nz):
        to = lax.rem(z + d, nz)
        copy = remote(row_ref.at[to], land1.at[z], send1.at[d - 1], recv1.at[d - 1], blk=to * nq + q)
        copy.start()
        stage1.append(copy)
    land1[pl.ds(z, 1)] = row_ref[pl.ds(z, 1)]

    ordered, last = sort_slots(pairs_v[...], order_v[...], me * fb)
    ordered_v[...] = ordered
    last_v[...] = last
    metas = [
        pltpu.make_async_copy(ordered_v, ordered_s, meta_sem.at[0]),
        pltpu.make_async_copy(last_v, last_s, meta_sem.at[1]),
    ]
    for copy in metas:
        copy.start()

    for copy in stage1:
        copy.wait_recv()
    stage2 = []
    for d in (4, 3, 5, 2, 6, 1, 7)[:] if nq == 8 else range(1, nq):
        to = lax.rem(q + d, nq)
        copy = remote(land1.at[:, to], gathered.at[q], send2.at[d - 1], recv2.at[d - 1], blk=z * nq + to)
        copy.start()
        stage2.append(copy)
    gathered[pl.ds(q, 1)] = land1[:, pl.ds(q, 1)].reshape(1, nz, fb, LANES)
    for copy in metas:
        copy.wait()
    for load in loads:
        load.wait()
    for copy in stage2:
        copy.wait_recv()
    by_factor = jnp.swapaxes(gathered[...].reshape(rows, fb, LANES).astype(F32), 0, 1)
    shocks_b[...] = by_factor.astype(BF16)

    unroll = min(64, slots)
    slot_bits = slots.bit_length() - 1

    def slot_group(g, carry):
        total, before = carry
        for u in range(unroll):
            j = g * unroll + u
            value = ordered_s[0, j]
            factor = value & 3
            k = (value >> 2) & (slots - 1)
            position = value >> (2 + slot_bits)
            product = jnp.dot(shocks_b[factor], sens_v[k], preferred_element_type=F32)
            same = (position == before).astype(F32)
            total = total * same + product
            running[j] = total
            before = position
        return total, before

    lax.fori_loop(0, slots // unroll, slot_group, (jnp.zeros((rows, LANES), F32), jnp.int32(-1)))

    def partial_of(p):
        value = last_s[0, p]
        return running[(value >> 1) & (slots - 1)] * (value & 1).astype(F32)

    chunks = len(dz_order)
    core_copies, x_copies, z_copies = [], [], []
    for i, dz in enumerate(dz_order):
        to_z = lax.rem(z + dz, nz)
        for to_x in range(NX):
            for h in range(2):
                give[i, to_x, h] = partial_of(((to_z * NX + to_x) * NC + (1 - c)) * 2 + h)
        copy = remote(give.at[i], got0.at[i], send_c.at[i], recv_c.at[i], blk=z * nq + x * NC + (1 - c))
        copy.start()
        core_copies.append(copy)

    right = (z * NX + lax.rem(x + 1, NX)) * NC + c
    left = (z * NX + lax.rem(x + NX - 1, NX)) * NC + c
    relays, rest_copies, last_copies = [], [], []
    top = mine.shape[2]
    for i, dz in enumerate(dz_order):
        to_z = lax.rem(z + dz, nz)
        core_copies[i].wait_recv()
        pair = []
        for d in (2, 1, 3, 0):
            to_x = lax.rem(x + d, NX)
            for h in range(2):
                both = got0[i, to_x, h] + partial_of(((to_z * NX + to_x) * NC + c) * 2 + h)
                total, rest = both[:top], both[top:]
                if dz == 0:
                    rest_own[to_x, h] = rest
                else:
                    rest_z[i, to_x, h] = rest.astype(BF16)
                if d == 0:
                    mine[i, h] = total
                elif d == 2:
                    part_r[i, h] = total.astype(BF16)
                    copy = remote(
                        part_r.at[i, h], got_r.at[i, h], send_r.at[i, h], recv_r.at[i, h], blk=left if h else right
                    )
                    copy.start()
                    pair.append(copy)
                else:
                    held[i, d // 2, h] = total
        if dz != 0:
            copy = remote(rest_z.at[i], got_v.at[i], send_v.at[i], recv_v.at[i], blk=to_z * nq + q)
            copy.start()
            rest_copies.append(copy)
        relays.append(pair)

    for i in range(chunks):
        for copy in relays[i]:
            copy.wait_recv()
        group = []
        for way in range(2):
            for h in range(2):
                total = held[i, way, h]
                if h == way:
                    total = total + got_r[i, h].astype(F32)
                part_x[i, way, h] = total.astype(BF16)
            copy = remote(
                part_x.at[i, way], got1.at[i, way], send_x.at[i, way], recv_x.at[i, way], blk=left if way else right
            )
            copy.start()
            group.append(copy)
        x_copies.append(group)

    for i, dz in enumerate(dz_order):
        for copy in x_copies[i]:
            copy.wait_recv()
        for h in range(2):
            total = mine[i, h]
            for way in range(2):
                total = total + got1[i, way, h].astype(F32)
            if dz == 0:
                mine[i, h] = total
            else:
                part_z[i, h] = total.astype(BF16)
        if dz != 0:
            copy = remote(
                part_z.at[i], got2.at[i], send_z.at[i], recv_z.at[i], blk=lax.rem(z + dz, nz) * nq + q
            )
            copy.start()
            z_copies.append(copy)
        if i == nz // 2 - 1:
            for copy in rest_copies:
                copy.wait_recv()
            for d in (2, 1, 3, 0):
                to_x = lax.rem(x + d, NX)
                for h in range(2):
                    total = rest_own[to_x, h]
                    for e in range(chunks - 1):
                        total = total + got_v[e, to_x, h].astype(F32)
                    if d == 0:
                        rest_mine[h] = total
                    else:
                        rest_x[d - 1, h] = total.astype(BF16)
                if d > 0:
                    copy = remote(
                        rest_x.at[d - 1], got_w.at[d - 1], send_w.at[d - 1], recv_w.at[d - 1],
                        blk=(z * NX + to_x) * NC + c,
                    )
                    copy.start()
                    last_copies.append(copy)
    for copy in last_copies + z_copies:
        copy.wait_recv()
    for h in range(2):
        total = mine[chunks - 1, h]
        for e in range(chunks - 1):
            total = total + got2[e, h].astype(F32)
        rest = rest_mine[h]
        for d in range(NX - 1):
            rest = rest + got_w[d, h].astype(F32)
        total = jnp.concatenate([total, rest], axis=0)
        squares[0, h:h + 1] = jnp.sum(total * total, axis=0, keepdims=True)
        total = jnp.swapaxes(total.reshape(nq, nz, LANES), 0, 1)
        out_ref[:, h * LANES:(h + 1) * LANES] = total.reshape(rows, LANES)
    save = pltpu.make_async_copy(out_ref, out_hbm, out_sem.at[0])
    y_copies = []
    for d in far_first(ny):
        copy = remote(
            squares.at[0], got3.at[d - 1], send_y.at[d - 1], recv_y.at[d - 1], scen=lax.rem(me_y + d, ny)
        )
        copy.start()
        y_copies.append(copy)
    save.start()
    for copy in y_copies:
        copy.wait_recv()
    total = squares[0]
    for d in range(ny - 1):
        total = total + got3[d]
    rms_ref[...] = jnp.sqrt(total / (rows * ny) + 1e-06)
    save_rms = pltpu.make_async_copy(rms_ref, rms_hbm, out_sem.at[1])
    save_rms.start()
    for copy in stage1 + stage2 + core_copies + rest_copies + last_copies + z_copies + y_copies:
        copy.wait_send()
    for group in relays + x_copies:
        for copy in group:
            copy.wait_send()
    save.wait()
    save_rms.wait()


def shards(ny, nz, returns, vol_hist, vol_now, sensitivity, block_pairs, book_order):
    nq = NX * NC
    slots = sensitivity.shape[0]
    blocks = book_order.shape[0]
    factors = returns.shape[1]
    rows = nz * nq
    fb = factors // (rows * LANES)
    wide = (rows, fb, LANES)
    hbm = (pl.BlockSpec(memory_space=pltpu.HBM),) * 6
    dma = pltpu.SemaphoreType.DMA
    vm = pltpu.VMEM
    block = (rows, LANES)
    upper, lower = (rows - rows // 4, LANES), (rows // 4, LANES)
    shapes = (jax.ShapeDtypeStruct((rows, 2 * LANES), F32), jax.ShapeDtypeStruct((2, LANES), F32))
    out, rms = pl.pallas_call(
        functools.partial(kernel, ny, nz, far_first(nz) + [0]),
        out_shape=shapes,
        in_specs=hbm,
        out_specs=hbm[:2],
        scratch_shapes=[
            vm((rows, 2 * LANES), F32),
            vm((2, LANES), F32),
            vm((1, factors), BF16),
            vm(wide, F32),
            vm(wide, F32),
            vm((3, slots), jnp.int32),
            vm((1, blocks), jnp.int32),
            vm(wide, F32),
            vm((nz, nq, fb, LANES), BF16),
            vm((slots, LANES, LANES), BF16),
            vm((nz, nq, fb, LANES), BF16),
            vm((nq, nz, fb, LANES), BF16),
            vm((fb,) + block, BF16),
            vm((slots,) + block, F32),
            vm((nz, NX, 2) + block, F32),
            vm((nz, NX, 2) + block, F32),
            vm((nz, 2) + upper, BF16),
            vm((nz, 2) + upper, BF16),
            vm((nz, 2, 2) + upper, F32),
            vm((nz, 2, 2) + upper, BF16),
            vm((nz, 2, 2) + upper, BF16),
            vm((nz - 1, 2) + upper, BF16),
            vm((nz - 1, 2) + upper, BF16),
            vm((nz, 2) + upper, F32),
            vm((nz - 1, NX, 2) + lower, BF16),
            vm((nz - 1, NX, 2) + lower, BF16),
            vm((NX, 2) + lower, F32),
            vm((2,) + lower, F32),
            vm((NX - 1, 2) + lower, BF16),
            vm((NX - 1, 2) + lower, BF16),
            vm((1, 2, LANES), F32),
            vm((ny - 1, 2, LANES), F32),
            vm((1, slots), jnp.int32),
            vm((1, blocks), jnp.int32),
            pltpu.SMEM((1, slots), jnp.int32),
            pltpu.SMEM((1, blocks), jnp.int32),
            dma((5,)),
            dma((2,)),
            dma((8,)),
            dma((2,)),
            dma((nz - 1,)),
            dma((nz - 1,)),
            dma((nq - 1,)),
            dma((nq - 1,)),
            dma((nz,)),
            dma((nz,)),
            dma((nz, 2)),
            dma((nz, 2)),
            dma((nz, 2)),
            dma((nz, 2)),
            dma((nz - 1,)),
            dma((nz - 1,)),
            dma((nz - 1,)),
            dma((nz - 1,)),
            dma((NX - 1,)),
            dma((NX - 1,)),
            dma((ny - 1,)),
            dma((ny - 1,)),
        ],
        compiler_params=pltpu.CompilerParams(
            collective_id=0, has_side_effects=True, vmem_limit_bytes=60 << 20
        ),
        name="profit_loss",
    )(
        returns, vol_hist.reshape(wide), vol_now.reshape(wide), block_pairs.T, book_order.reshape(1, blocks), sensitivity
    )
    return out, rms.reshape(2 * LANES)


def solution(mesh):
    ny, nb = mesh.shape["scen"], mesh.shape["blk"]
    return jax.shard_map(
        functools.partial(shards, ny, nb // (NX * NC)),
        mesh=mesh,
        in_specs=(
            P(("scen", "blk"), None),
            P(("scen", "blk"), None),
            P(),
            P("blk", None, None),
            P("blk", None),
            P(),
        ),
        out_specs=(P("scen", "blk"), P("blk")),
        check_vma=False,
    )
```

```python
import functools

import jax
import jax.numpy as jnp
from jax import lax
from jax.experimental import pallas as pl
from jax.experimental.pallas import tpu as pltpu
from jax.sharding import PartitionSpec as P

MESH = pl.DeviceIdType.MESH
F32 = jnp.float32
BF16 = jnp.bfloat16
NX = 4
NC = 2
LANES = 128


def remote(src, dst, send, recv, **where):
    return pltpu.make_async_remote_copy(
        src_ref=src, dst_ref=dst, send_sem=send, recv_sem=recv, device_id=where, device_id_type=MESH
    )


def far_first(n):
    return sorted(range(1, n), key=lambda d: (-min(d, n - d), d))


def iota(shape, axis):
    return lax.broadcasted_iota(jnp.int32, shape, axis).astype(F32)


def to_column(row):
    n = row.shape[1]
    eye = lax.broadcasted_iota(jnp.int32, (n, n), 0) == lax.broadcasted_iota(jnp.int32, (n, n), 1)
    return jnp.sum(jnp.where(eye, jnp.broadcast_to(row, (n, n)), 0.0), axis=1, keepdims=True)


def sort_slots(pairs, order, first_factor):
    slots, blocks = pairs.shape[1], order.shape[1]
    pairs = pairs.astype(F32)
    factor = pairs[0:1] - first_factor.astype(F32)
    matches = to_column(order.astype(F32)) == pairs[1:2]
    position = jnp.sum(jnp.where(matches, iota((blocks, slots), 0), 0.0), axis=0, keepdims=True)
    position = jnp.where(pairs[2:3] > 0.5, position, float(blocks))
    value = (position * slots + iota((1, slots), 1)) * 4.0 + factor
    value_col = to_column(value)
    position_col = to_column(position)
    rank_col = jnp.sum(jnp.where(value < value_col, 1.0, 0.0), axis=1, keepdims=True)
    ordered = jnp.sum(jnp.where(rank_col == iota((slots, slots), 1), value_col, 0.0), axis=0, keepdims=True)
    columns = iota((slots, blocks), 1)
    upto = jnp.sum(jnp.where(position_col <= columns, 1.0, 0.0), axis=0, keepdims=True)
    here = jnp.sum(jnp.where(position_col == columns, 1.0, 0.0), axis=0, keepdims=True)
    last = jnp.maximum(upto - 1.0, 0.0) * 2.0 + jnp.minimum(here, 1.0)
    return ordered.astype(jnp.int32), last.astype(jnp.int32)


def kernel(
    ny, nz, dz_order,
    returns_ref, hist_ref, now_ref, slots_ref, sens_ref,
    out_hbm, rms_hbm,
    out_ref, rms_ref, returns_v, hist_v, now_v, slots_v, wide, row_ref,
    sens_v, land1, gathered, shocks_b, running, give, got0, part_r, got_r, held, part_x, got1, part_z, got2, mine, rest_z, got_v, rest_own, rest_mine, rest_x, got_w,
    squares, got3, ordered_v, last_v, ordered_s, last_s,
    in_sem, out_sem, sens_sem, meta_sem, send1, recv1, send2, recv2, send_c, recv_c, send_r, recv_r, send_x, recv_x, send_z, recv_z, send_v, recv_v, send_w, recv_w, send_y, recv_y,
):
    nq = NX * NC
    slots = sens_v.shape[0]
    rows = nz * nq
    me_y = lax.axis_index("scen")
    me = lax.axis_index("blk")
    z, q = me // nq, me % nq
    x, c = q // NC, q % NC
    fb = shocks_b.shape[0]

    inputs = [
        pltpu.make_async_copy(src, dst, in_sem.at[i])
        for i, (src, dst) in enumerate((
            (returns_ref, returns_v), (hist_ref, hist_v), (now_ref, now_v), (slots_ref, slots_v)
        ))
    ]
    for copy in inputs:
        copy.start()
    barrier = pltpu.get_barrier_semaphore()
    for d in far_first(nz):
        pl.semaphore_signal(barrier, 1, device_id={"blk": lax.rem(z + d, nz) * nq + q}, device_id_type=MESH)
    for d in far_first(ny):
        pl.semaphore_signal(barrier, 1, device_id={"scen": lax.rem(me_y + d, ny)}, device_id_type=MESH)
    for d in range(1, nq):
        pl.semaphore_signal(barrier, 1, device_id={"blk": z * nq + lax.rem(q + d, nq)}, device_id_type=MESH)

    pieces = sens_sem.shape[0]
    each = slots // pieces
    loads = [
        pltpu.make_async_copy(sens_ref.at[pl.ds(i * each, each)], sens_v.at[pl.ds(i * each, each)], sens_sem.at[i])
        for i in range(pieces)
    ]
    for copy in inputs:
        copy.wait()

    def rescale(to):
        part = pl.ds(to * nq, nq)
        for i in range(nq * fb):
            start = pl.multiple_of((to * nq * fb + i) * LANES, LANES)
            wide[i // fb, i % fb:i % fb + 1] = returns_v[:, pl.ds(start, LANES)].astype(F32)
        row_ref[to] = (wide[...] * now_v[part] / hist_v[part]).astype(BF16)

    for d in far_first(nz)[:3]:
        rescale(lax.rem(z + d, nz))

    pl.semaphore_wait(barrier, nz - 1 + nq - 1 + ny - 1)

    stage1 = []
    for n, d in enumerate(far_first(nz)):
        to = lax.rem(z + d, nz)
        if n > 2:
            rescale(to)
        copy = remote(row_ref.at[to], land1.at[z], send1.at[d - 1], recv1.at[d - 1], blk=to * nq + q)
        copy.start()
        stage1.append(copy)
    rescale(z)
    land1[pl.ds(z, 1)] = row_ref[pl.ds(z, 1)]
    for load in loads:
        load.start()

    ordered, last = sort_slots(slots_v[0:3], slots_v[3:4, :last_v.shape[1]], me * fb)
    ordered_v[...] = ordered
    last_v[...] = last
    metas = [
        pltpu.make_async_copy(ordered_v, ordered_s, meta_sem.at[0]),
        pltpu.make_async_copy(last_v, last_s, meta_sem.at[1]),
    ]
    for copy in metas:
        copy.start()

    for copy in stage1:
        copy.wait_recv()
    stage2 = []
    for d in (4, 3, 5, 2, 6, 1, 7)[:] if nq == 8 else range(1, nq):
        to = lax.rem(q + d, nq)
        copy = remote(land1.at[:, to], gathered.at[q], send2.at[d - 1], recv2.at[d - 1], blk=z * nq + to)
        copy.start()
        stage2.append(copy)
    gathered[pl.ds(q, 1)] = land1[:, pl.ds(q, 1)].reshape(1, nz, fb, LANES)
    for copy in metas:
        copy.wait()
    for load in loads:
        load.wait()
    for copy in stage2:
        copy.wait_recv()
    by_factor = jnp.swapaxes(gathered[...].reshape(rows, fb, LANES).astype(F32), 0, 1)
    shocks_b[...] = by_factor.astype(BF16)

    unroll = min(128, slots)
    slot_bits = slots.bit_length() - 1

    def slot_group(g, carry):
        total, before = carry
        for u in range(unroll):
            j = g * unroll + u
            value = ordered_s[0, j]
            factor = value & 3
            k = (value >> 2) & (slots - 1)
            position = value >> (2 + slot_bits)
            product = jnp.dot(shocks_b[factor], sens_v[k], preferred_element_type=F32)
            same = (position == before).astype(F32)
            total = total * same + product
            running[j] = total
            before = position
        return total, before

    lax.fori_loop(0, slots // unroll, slot_group, (jnp.zeros((rows, LANES), F32), jnp.int32(-1)))

    def partial_of(p):
        value = last_s[0, p]
        return running[(value >> 1) & (slots - 1)] * (value & 1).astype(F32)

    chunks = len(dz_order)
    core_copies, x_copies, z_copies = [], [], []
    for i, dz in enumerate(dz_order):
        to_z = lax.rem(z + dz, nz)
        for to_x in range(NX):
            for h in range(2):
                give[i, to_x, h] = partial_of(((to_z * NX + to_x) * NC + (1 - c)) * 2 + h)
        copy = remote(give.at[i], got0.at[i], send_c.at[i], recv_c.at[i], blk=z * nq + x * NC + (1 - c))
        copy.start()
        core_copies.append(copy)

    right = (z * NX + lax.rem(x + 1, NX)) * NC + c
    left = (z * NX + lax.rem(x + NX - 1, NX)) * NC + c
    relays, rest_copies, last_copies = [], [], []
    top = mine.shape[2]
    for i, dz in enumerate(dz_order):
        to_z = lax.rem(z + dz, nz)
        core_copies[i].wait_recv()
        pair = []
        for d in (2, 1, 3, 0):
            to_x = lax.rem(x + d, NX)
            for h in range(2):
                both = got0[i, to_x, h] + partial_of(((to_z * NX + to_x) * NC + c) * 2 + h)
                total, rest = both[:top], both[top:]
                if dz == 0:
                    rest_own[to_x, h] = rest
                else:
                    rest_z[i, to_x, h] = rest.astype(BF16)
                if d == 0:
                    mine[i, h] = total
                elif d == 2:
                    part_r[i, h] = total.astype(BF16)
                    copy = remote(
                        part_r.at[i, h], got_r.at[i, h], send_r.at[i, h], recv_r.at[i, h], blk=left if h else right
                    )
                    copy.start()
                    pair.append(copy)
                else:
                    held[i, d // 2, h] = total
        if dz != 0:
            copy = remote(rest_z.at[i], got_v.at[i], send_v.at[i], recv_v.at[i], blk=to_z * nq + q)
            copy.start()
            rest_copies.append(copy)
        relays.append(pair)

    for i in range(chunks):
        for copy in relays[i]:
            copy.wait_recv()
        group = []
        for way in range(2):
            for h in range(2):
                total = held[i, way, h]
                if h == way:
                    total = total + got_r[i, h].astype(F32)
                part_x[i, way, h] = total.astype(BF16)
            copy = remote(
                part_x.at[i, way], got1.at[i, way], send_x.at[i, way], recv_x.at[i, way], blk=left if way else right
            )
            copy.start()
            group.append(copy)
        x_copies.append(group)

    for i, dz in enumerate(dz_order):
        for copy in x_copies[i]:
            copy.wait_recv()
        for h in range(2):
            total = mine[i, h]
            for way in range(2):
                total = total + got1[i, way, h].astype(F32)
            if dz == 0:
                mine[i, h] = total
            else:
                part_z[i, h] = total.astype(BF16)
        if dz != 0:
            copy = remote(
                part_z.at[i], got2.at[i], send_z.at[i], recv_z.at[i], blk=lax.rem(z + dz, nz) * nq + q
            )
            copy.start()
            z_copies.append(copy)
        if i == nz // 2 - 1:
            for copy in rest_copies:
                copy.wait_recv()
            for d in (2, 1, 3, 0):
                to_x = lax.rem(x + d, NX)
                for h in range(2):
                    total = rest_own[to_x, h]
                    for e in range(chunks - 1):
                        total = total + got_v[e, to_x, h].astype(F32)
                    if d == 0:
                        rest_mine[h] = total
                    else:
                        rest_x[d - 1, h] = total.astype(BF16)
                if d > 0:
                    copy = remote(
                        rest_x.at[d - 1], got_w.at[d - 1], send_w.at[d - 1], recv_w.at[d - 1],
                        blk=(z * NX + to_x) * NC + c,
                    )
                    copy.start()
                    last_copies.append(copy)
    for copy in last_copies + z_copies:
        copy.wait_recv()
    for h in range(2):
        total = mine[chunks - 1, h]
        for e in range(chunks - 1):
            total = total + got2[e, h].astype(F32)
        rest = rest_mine[h]
        for d in range(NX - 1):
            rest = rest + got_w[d, h].astype(F32)
        total = jnp.concatenate([total, rest], axis=0)
        squares[0, h:h + 1] = jnp.sum(total * total, axis=0, keepdims=True)
        total = jnp.swapaxes(total.reshape(nq, nz, LANES), 0, 1)
        out_ref[:, h * LANES:(h + 1) * LANES] = total.reshape(rows, LANES)
    save = pltpu.make_async_copy(out_ref, out_hbm, out_sem.at[0])
    y_copies = []
    for d in far_first(ny):
        copy = remote(
            squares.at[0], got3.at[d - 1], send_y.at[d - 1], recv_y.at[d - 1], scen=lax.rem(me_y + d, ny)
        )
        copy.start()
        y_copies.append(copy)
    save.start()
    for copy in y_copies:
        copy.wait_recv()
    total = squares[0]
    for d in range(ny - 1):
        total = total + got3[d]
    rms_ref[...] = jnp.sqrt(total / (rows * ny) + 1e-06)
    save_rms = pltpu.make_async_copy(rms_ref, rms_hbm, out_sem.at[1])
    save_rms.start()
    for copy in stage1 + stage2 + core_copies + rest_copies + last_copies + z_copies + y_copies:
        copy.wait_send()
    for group in relays + x_copies:
        for copy in group:
            copy.wait_send()
    save.wait()
    save_rms.wait()


def shards(ny, nz, returns, vol_hist, vol_now, sensitivity, block_pairs, book_order):
    nq = NX * NC
    slots = sensitivity.shape[0]
    blocks = book_order.shape[0]
    factors = returns.shape[1]
    rows = nz * nq
    fb = factors // (rows * LANES)
    wide = (rows, fb, LANES)
    table = jnp.pad(block_pairs.T, ((0, 1), (0, 0))) + jnp.pad(book_order[None], ((3, 0), (0, slots - blocks)))
    hbm = (pl.BlockSpec(memory_space=pltpu.HBM),) * 5
    dma = pltpu.SemaphoreType.DMA
    vm = pltpu.VMEM
    block = (rows, LANES)
    upper, lower = (rows - rows // 4, LANES), (rows // 4, LANES)
    shapes = (jax.ShapeDtypeStruct((rows, 2 * LANES), F32), jax.ShapeDtypeStruct((2, LANES), F32))
    out, rms = pl.pallas_call(
        functools.partial(kernel, ny, nz, far_first(nz) + [0]),
        out_shape=shapes,
        in_specs=hbm,
        out_specs=hbm[:2],
        scratch_shapes=[
            vm((rows, 2 * LANES), F32),
            vm((2, LANES), F32),
            vm((1, factors), BF16),
            vm(wide, F32),
            vm(wide, F32),
            vm((4, slots), jnp.int32),
            vm((nq, fb, LANES), F32),
            vm((nz, nq, fb, LANES), BF16),
            vm((slots, LANES, LANES), BF16),
            vm((nz, nq, fb, LANES), BF16),
            vm((nq, nz, fb, LANES), BF16),
            vm((fb,) + block, BF16),
            vm((slots,) + block, F32),
            vm((nz, NX, 2) + block, F32),
            vm((nz, NX, 2) + block, F32),
            vm((nz, 2) + upper, BF16),
            vm((nz, 2) + upper, BF16),
            vm((nz, 2, 2) + upper, F32),
            vm((nz, 2, 2) + upper, BF16),
            vm((nz, 2, 2) + upper, BF16),
            vm((nz - 1, 2) + upper, BF16),
            vm((nz - 1, 2) + upper, BF16),
            vm((nz, 2) + upper, F32),
            vm((nz - 1, NX, 2) + lower, BF16),
            vm((nz - 1, NX, 2) + lower, BF16),
            vm((NX, 2) + lower, F32),
            vm((2,) + lower, F32),
            vm((NX - 1, 2) + lower, BF16),
            vm((NX - 1, 2) + lower, BF16),
            vm((1, 2, LANES), F32),
            vm((ny - 1, 2, LANES), F32),
            vm((1, slots), jnp.int32),
            vm((1, blocks), jnp.int32),
            pltpu.SMEM((1, slots), jnp.int32),
            pltpu.SMEM((1, blocks), jnp.int32),
            dma((4,)),
            dma((2,)),
            dma((8,)),
            dma((2,)),
            dma((nz - 1,)),
            dma((nz - 1,)),
            dma((nq - 1,)),
            dma((nq - 1,)),
            dma((nz,)),
            dma((nz,)),
            dma((nz, 2)),
            dma((nz, 2)),
            dma((nz, 2)),
            dma((nz, 2)),
            dma((nz - 1,)),
            dma((nz - 1,)),
            dma((nz - 1,)),
            dma((nz - 1,)),
            dma((NX - 1,)),
            dma((NX - 1,)),
            dma((ny - 1,)),
            dma((ny - 1,)),
        ],
        compiler_params=pltpu.CompilerParams(
            collective_id=0, has_side_effects=True, vmem_limit_bytes=56448000
        ),
        name="profit_loss",
    )(
        returns, vol_hist.reshape(wide), vol_now.reshape(wide), table, sensitivity
    )
    return out, rms.reshape(2 * LANES)


def solution(mesh):
    ny, nb = mesh.shape["scen"], mesh.shape["blk"]
    return jax.shard_map(
        functools.partial(shards, ny, nb // (NX * NC)),
        mesh=mesh,
        in_specs=(
            P(("scen", "blk"), None),
            P(("scen", "blk"), None),
            P(),
            P("blk", None, None),
            P("blk", None),
            P(),
        ),
        out_specs=(P("scen", "blk"), P("blk")),
        check_vma=False,
    )
```

```python
import functools

import jax
import jax.numpy as jnp
from jax import lax
from jax.experimental import pallas as pl
from jax.experimental.pallas import tpu as pltpu
from jax.sharding import PartitionSpec as P

MESH = pl.DeviceIdType.MESH
F32 = jnp.float32
BF16 = jnp.bfloat16
NX = 4
NC = 2
LANES = 128


def remote(src, dst, send, recv, **where):
    return pltpu.make_async_remote_copy(
        src_ref=src, dst_ref=dst, send_sem=send, recv_sem=recv, device_id=where, device_id_type=MESH
    )


def far_first(n):
    return sorted(range(1, n), key=lambda d: (-min(d, n - d), d))


def iota(shape, axis):
    return lax.broadcasted_iota(jnp.int32, shape, axis).astype(F32)


def to_column(row):
    n = row.shape[1]
    eye = lax.broadcasted_iota(jnp.int32, (n, n), 0) == lax.broadcasted_iota(jnp.int32, (n, n), 1)
    return jnp.sum(jnp.where(eye, jnp.broadcast_to(row, (n, n)), 0.0), axis=1, keepdims=True)


def sort_slots(pairs, order, first_factor):
    slots, blocks = pairs.shape[1], order.shape[1]
    pairs = pairs.astype(F32)
    factor = pairs[0:1] - first_factor.astype(F32)
    matches = to_column(order.astype(F32)) == pairs[1:2]
    position = jnp.sum(jnp.where(matches, iota((blocks, slots), 0), 0.0), axis=0, keepdims=True)
    position = jnp.where(pairs[2:3] > 0.5, position, float(blocks))
    value = (position * slots + iota((1, slots), 1)) * 4.0 + factor
    value_col = to_column(value)
    position_col = to_column(position)
    rank_col = jnp.sum(jnp.where(value < value_col, 1.0, 0.0), axis=1, keepdims=True)
    ordered = jnp.sum(jnp.where(rank_col == iota((slots, slots), 1), value_col, 0.0), axis=0, keepdims=True)
    columns = iota((slots, blocks), 1)
    upto = jnp.sum(jnp.where(position_col <= columns, 1.0, 0.0), axis=0, keepdims=True)
    here = jnp.sum(jnp.where(position_col == columns, 1.0, 0.0), axis=0, keepdims=True)
    last = jnp.maximum(upto - 1.0, 0.0) * 2.0 + jnp.minimum(here, 1.0)
    return ordered.astype(jnp.int32), last.astype(jnp.int32)


def kernel(
    ny, nz, dz_order,
    returns_ref, hist_ref, now_ref, slots_ref, sens_ref,
    out_ref, rms_ref,
    returns_v, hist_v, now_v, slots_v, wide, row_ref,
    sens_v, land1, gathered, shocks_b, running, give, got0, part_r, got_r, held, part_x, got1, part_z, got2, mine, rest_z, got_v, rest_own, rest_mine, rest_x, got_w,
    squares, got3, ordered_v, last_v, ordered_s, last_s,
    in_sem, sens_sem, meta_sem, send1, recv1, send2, recv2, send_c, recv_c, send_r, recv_r, send_x, recv_x, send_z, recv_z, send_v, recv_v, send_w, recv_w, send_y, recv_y,
):
    nq = NX * NC
    slots = sens_v.shape[0]
    rows = nz * nq
    me_y = lax.axis_index("scen")
    me = lax.axis_index("blk")
    z, q = me // nq, me % nq
    x, c = q // NC, q % NC
    fb = shocks_b.shape[0]

    inputs = [
        pltpu.make_async_copy(src, dst, in_sem.at[i])
        for i, (src, dst) in enumerate((
            (returns_ref, returns_v), (hist_ref, hist_v), (now_ref, now_v), (slots_ref, slots_v)
        ))
    ]
    for copy in inputs:
        copy.start()
    barrier = pltpu.get_barrier_semaphore()
    for d in far_first(nz):
        pl.semaphore_signal(barrier, 1, device_id={"blk": lax.rem(z + d, nz) * nq + q}, device_id_type=MESH)
    for d in far_first(ny):
        pl.semaphore_signal(barrier, 1, device_id={"scen": lax.rem(me_y + d, ny)}, device_id_type=MESH)
    for d in range(1, nq):
        pl.semaphore_signal(barrier, 1, device_id={"blk": z * nq + lax.rem(q + d, nq)}, device_id_type=MESH)

    pieces = sens_sem.shape[0]
    each = slots // pieces
    loads = [
        pltpu.make_async_copy(sens_ref.at[pl.ds(i * each, each)], sens_v.at[pl.ds(i * each, each)], sens_sem.at[i])
        for i in range(pieces)
    ]
    for copy in inputs:
        copy.wait()

    def rescale(to):
        part = pl.ds(to * nq, nq)
        for i in range(nq * fb):
            start = pl.multiple_of((to * nq * fb + i) * LANES, LANES)
            wide[i // fb, i % fb:i % fb + 1] = returns_v[:, pl.ds(start, LANES)].astype(F32)
        row_ref[to] = (wide[...] * now_v[part] / hist_v[part]).astype(BF16)

    for d in far_first(nz)[:3]:
        rescale(lax.rem(z + d, nz))

    pl.semaphore_wait(barrier, nz - 1 + nq - 1 + ny - 1)

    stage1 = []
    for n, d in enumerate(far_first(nz)):
        to = lax.rem(z + d, nz)
        if n > 2:
            rescale(to)
        copy = remote(row_ref.at[to], land1.at[z], send1.at[d - 1], recv1.at[d - 1], blk=to * nq + q)
        copy.start()
        stage1.append(copy)
    rescale(z)
    land1[pl.ds(z, 1)] = row_ref[pl.ds(z, 1)]
    for load in loads:
        load.start()

    ordered, last = sort_slots(slots_v[0:3], slots_v[3:4, :last_v.shape[1]], me * fb)
    ordered_v[...] = ordered
    last_v[...] = last
    metas = [
        pltpu.make_async_copy(ordered_v, ordered_s, meta_sem.at[0]),
        pltpu.make_async_copy(last_v, last_s, meta_sem.at[1]),
    ]
    for copy in metas:
        copy.start()

    for copy in stage1:
        copy.wait_recv()
    stage2 = []
    for d in (4, 3, 5, 2, 6, 1, 7)[:] if nq == 8 else range(1, nq):
        to = lax.rem(q + d, nq)
        copy = remote(land1.at[:, to], gathered.at[q], send2.at[d - 1], recv2.at[d - 1], blk=z * nq + to)
        copy.start()
        stage2.append(copy)
    gathered[pl.ds(q, 1)] = land1[:, pl.ds(q, 1)].reshape(1, nz, fb, LANES)
    for copy in metas:
        copy.wait()
    for load in loads:
        load.wait()
    for copy in stage2:
        copy.wait_recv()
    by_factor = jnp.swapaxes(gathered[...].reshape(rows, fb, LANES).astype(F32), 0, 1)
    shocks_b[...] = by_factor.astype(BF16)

    unroll = min(128, slots)
    slot_bits = slots.bit_length() - 1

    def slot_group(g, carry):
        total, before = carry
        for u in range(unroll):
            j = g * unroll + u
            value = ordered_s[0, j]
            factor = value & 3
            k = (value >> 2) & (slots - 1)
            position = value >> (2 + slot_bits)
            product = jnp.dot(shocks_b[factor], sens_v[k], preferred_element_type=F32)
            same = (position == before).astype(F32)
            total = total * same + product
            running[j] = total
            before = position
        return total, before

    lax.fori_loop(0, slots // unroll, slot_group, (jnp.zeros((rows, LANES), F32), jnp.int32(-1)))

    def partial_of(p):
        value = last_s[0, p]
        return running[(value >> 1) & (slots - 1)] * (value & 1).astype(F32)

    chunks = len(dz_order)
    core_copies, x_copies, z_copies = [], [], []
    for i, dz in enumerate(dz_order):
        to_z = lax.rem(z + dz, nz)
        for to_x in range(NX):
            for h in range(2):
                give[i, to_x, h] = partial_of(((to_z * NX + to_x) * NC + (1 - c)) * 2 + h)
        copy = remote(give.at[i], got0.at[i], send_c.at[i], recv_c.at[i], blk=z * nq + x * NC + (1 - c))
        copy.start()
        core_copies.append(copy)

    right = (z * NX + lax.rem(x + 1, NX)) * NC + c
    left = (z * NX + lax.rem(x + NX - 1, NX)) * NC + c
    relays, rest_copies, last_copies = [], [], []
    top = mine.shape[2]
    for i, dz in enumerate(dz_order):
        to_z = lax.rem(z + dz, nz)
        core_copies[i].wait_recv()
        pair = []
        for d in (2, 1, 3, 0):
            to_x = lax.rem(x + d, NX)
            for h in range(2):
                both = got0[i, to_x, h] + partial_of(((to_z * NX + to_x) * NC + c) * 2 + h)
                total, rest = both[:top], both[top:]
                if dz == 0:
                    rest_own[to_x, h] = rest
                else:
                    rest_z[i, to_x, h] = rest.astype(BF16)
                if d == 0:
                    mine[i, h] = total
                elif d == 2:
                    part_r[i, h] = total.astype(BF16)
                    copy = remote(
                        part_r.at[i, h], got_r.at[i, h], send_r.at[i, h], recv_r.at[i, h], blk=left if h else right
                    )
                    copy.start()
                    pair.append(copy)
                else:
                    held[i, d // 2, h] = total
        if dz != 0:
            copy = remote(rest_z.at[i], got_v.at[i], send_v.at[i], recv_v.at[i], blk=to_z * nq + q)
            copy.start()
            rest_copies.append(copy)
        relays.append(pair)

    for i in range(chunks):
        for copy in relays[i]:
            copy.wait_recv()
        group = []
        for way in range(2):
            for h in range(2):
                total = held[i, way, h]
                if h == way:
                    total = total + got_r[i, h].astype(F32)
                part_x[i, way, h] = total.astype(BF16)
            copy = remote(
                part_x.at[i, way], got1.at[i, way], send_x.at[i, way], recv_x.at[i, way], blk=left if way else right
            )
            copy.start()
            group.append(copy)
        x_copies.append(group)

    for i, dz in enumerate(dz_order):
        for copy in x_copies[i]:
            copy.wait_recv()
        for h in range(2):
            total = mine[i, h]
            for way in range(2):
                total = total + got1[i, way, h].astype(F32)
            if dz == 0:
                mine[i, h] = total
            else:
                part_z[i, h] = total.astype(BF16)
        if dz != 0:
            copy = remote(
                part_z.at[i], got2.at[i], send_z.at[i], recv_z.at[i], blk=lax.rem(z + dz, nz) * nq + q
            )
            copy.start()
            z_copies.append(copy)
        if i == nz // 2 - 1:
            for copy in rest_copies:
                copy.wait_recv()
            for d in (2, 1, 3, 0):
                to_x = lax.rem(x + d, NX)
                for h in range(2):
                    total = rest_own[to_x, h]
                    for e in range(chunks - 1):
                        total = total + got_v[e, to_x, h].astype(F32)
                    if d == 0:
                        rest_mine[h] = total
                    else:
                        rest_x[d - 1, h] = total.astype(BF16)
                if d > 0:
                    copy = remote(
                        rest_x.at[d - 1], got_w.at[d - 1], send_w.at[d - 1], recv_w.at[d - 1],
                        blk=(z * NX + to_x) * NC + c,
                    )
                    copy.start()
                    last_copies.append(copy)
    for copy in last_copies + z_copies:
        copy.wait_recv()
    for h in range(2):
        total = mine[chunks - 1, h]
        for e in range(chunks - 1):
            total = total + got2[e, h].astype(F32)
        rest = rest_mine[h]
        for d in range(NX - 1):
            rest = rest + got_w[d, h].astype(F32)
        total = jnp.concatenate([total, rest], axis=0)
        squares[0, h:h + 1] = jnp.sum(total * total, axis=0, keepdims=True)
        total = jnp.swapaxes(total.reshape(nq, nz, LANES), 0, 1)
        out_ref[:, h * LANES:(h + 1) * LANES] = total.reshape(rows, LANES)
    y_copies = []
    for d in far_first(ny):
        copy = remote(
            squares.at[0], got3.at[d - 1], send_y.at[d - 1], recv_y.at[d - 1], scen=lax.rem(me_y + d, ny)
        )
        copy.start()
        y_copies.append(copy)
    for copy in stage1 + stage2 + core_copies + rest_copies + last_copies + z_copies + y_copies:
        copy.wait_send()
    for group in relays + x_copies:
        for copy in group:
            copy.wait_send()
    for copy in y_copies:
        copy.wait_recv()
    total = squares[0]
    for d in range(ny - 1):
        total = total + got3[d]
    rms_ref[...] = jnp.sqrt(total / (rows * ny) + 1e-06)


def shards(ny, nz, returns, vol_hist, vol_now, sensitivity, block_pairs, book_order):
    nq = NX * NC
    slots = sensitivity.shape[0]
    blocks = book_order.shape[0]
    factors = returns.shape[1]
    rows = nz * nq
    fb = factors // (rows * LANES)
    wide = (rows, fb, LANES)
    table = jnp.pad(block_pairs.T, ((0, 1), (0, 0))) + jnp.pad(book_order[None], ((3, 0), (0, slots - blocks)))
    hbm = (pl.BlockSpec(memory_space=pltpu.HBM),) * 5
    dma = pltpu.SemaphoreType.DMA
    vm = pltpu.VMEM
    block = (rows, LANES)
    upper, lower = (rows - rows // 4, LANES), (rows // 4, LANES)
    shapes = (jax.ShapeDtypeStruct((rows, 2 * LANES), F32), jax.ShapeDtypeStruct((2, LANES), F32))
    out, rms = pl.pallas_call(
        functools.partial(kernel, ny, nz, far_first(nz) + [0]),
        out_shape=shapes,
        in_specs=hbm,
        out_specs=(pl.BlockSpec(memory_space=pltpu.VMEM),) * 2,
        scratch_shapes=[
            vm((1, factors), BF16),
            vm(wide, F32),
            vm(wide, F32),
            vm((4, slots), jnp.int32),
            vm((nq, fb, LANES), F32),
            vm((nz, nq, fb, LANES), BF16),
            vm((slots, LANES, LANES), BF16),
            vm((nz, nq, fb, LANES), BF16),
            vm((nq, nz, fb, LANES), BF16),
            vm((fb,) + block, BF16),
            vm((slots,) + block, F32),
            vm((nz, NX, 2) + block, F32),
            vm((nz, NX, 2) + block, F32),
            vm((nz, 2) + upper, BF16),
            vm((nz, 2) + upper, BF16),
            vm((nz, 2, 2) + upper, F32),
            vm((nz, 2, 2) + upper, BF16),
            vm((nz, 2, 2) + upper, BF16),
            vm((nz - 1, 2) + upper, BF16),
            vm((nz - 1, 2) + upper, BF16),
            vm((nz, 2) + upper, F32),
            vm((nz - 1, NX, 2) + lower, BF16),
            vm((nz - 1, NX, 2) + lower, BF16),
            vm((NX, 2) + lower, F32),
            vm((2,) + lower, F32),
            vm((NX - 1, 2) + lower, BF16),
            vm((NX - 1, 2) + lower, BF16),
            vm((1, 2, LANES), F32),
            vm((ny - 1, 2, LANES), F32),
            vm((1, slots), jnp.int32),
            vm((1, blocks), jnp.int32),
            pltpu.SMEM((1, slots), jnp.int32),
            pltpu.SMEM((1, blocks), jnp.int32),
            dma((4,)),
            dma((8,)),
            dma((2,)),
            dma((nz - 1,)),
            dma((nz - 1,)),
            dma((nq - 1,)),
            dma((nq - 1,)),
            dma((nz,)),
            dma((nz,)),
            dma((nz, 2)),
            dma((nz, 2)),
            dma((nz, 2)),
            dma((nz, 2)),
            dma((nz - 1,)),
            dma((nz - 1,)),
            dma((nz - 1,)),
            dma((nz - 1,)),
            dma((NX - 1,)),
            dma((NX - 1,)),
            dma((ny - 1,)),
            dma((ny - 1,)),
        ],
        compiler_params=pltpu.CompilerParams(
            collective_id=0, has_side_effects=True, vmem_limit_bytes=56448000
        ),
        name="profit_loss",
    )(
        returns, vol_hist.reshape(wide), vol_now.reshape(wide), table, sensitivity
    )
    return out, rms.reshape(2 * LANES)


def solution(mesh):
    ny, nb = mesh.shape["scen"], mesh.shape["blk"]
    return jax.shard_map(
        functools.partial(shards, ny, nb // (NX * NC)),
        mesh=mesh,
        in_specs=(
            P(("scen", "blk"), None),
            P(("scen", "blk"), None),
            P(),
            P("blk", None, None),
            P("blk", None),
            P(),
        ),
        out_specs=(P("scen", "blk"), P("blk")),
        check_vma=False,
    )
```
